32 devices in a mesh: sec: 8 (over y, x, core), tp: 4 (over z).
Axes of the slice: x: 2, y: 2, z: 4, core: 2. Of those that a mesh axis runs over, the one named last changes fastest.
Arguments:
- queries: bfloat16 [8, 512, 4096], P('sec', 'tp'), may hold values from -5 to 5
- key_rows: bfloat16 [8, 512, 4096], P('sec', 'tp'), may hold values from -5 to 5
- value_rows: bfloat16 [8, 512, 4096], P('sec', 'tp'), may hold values from -6 to 6
- doc_ids: int32 [8, 512], P('sec'), may hold values from 0 to 15, never falling along the last dimension, each value on 1 to 64 neighbouring positions
- rewards: float32 [8, 512], P('sec', 'tp'), may hold values from -12 to 12
- value_head: float32 [4096], replicated, may hold values from -0.375 to 0.375
Outputs:
- attended: bfloat16 [8, 512, 4096], P('sec', 'tp')
- advantages: float32 [8, 512], P('sec', 'tp')
The draws below stay inside these ranges and needn't reach their ends.
Inputs may be any that keep to these rules, and one draw needn't show every extreme that they name: `doc_ids`: document numbers never fall along a micro-batch, each document spans 1 to 64 tokens, and some document exactly that many.
All inputs are finite; a program needn't handle non-finite values.
Results may differ from the reference program's by a relative error of at most 0.0023.
Values may be sent and summed in bfloat16 or wider, within the bound.
A program may use at most 64 MiB of HBM per device.

```python
import math
from functools import partial
import jax
import jax.numpy as jnp
import numpy as np
from jax import lax

HEAD = 128
HEADS = 32
FEAT = 4096
TOK_DEV = 128
TOKENS = 512
MICRO = 8
N_TP = 4


def drawn_pair(key):
    shape = (MICRO, TOKENS, FEAT)
    base_query = jnp.clip(jax.random.normal(jax.random.fold_in(key, 11), shape, jnp.float32), -4.5, 4.5)
    base_key = jnp.clip(jax.random.normal(jax.random.fold_in(key, 12), shape, jnp.float32), -4.5, 4.5)
    return (base_query, base_key)


def draw_queries(key, part):
    return drawn_pair(key)[0].astype(jnp.bfloat16)


def draw_key_rows(key, part):
    return drawn_pair(key)[1].astype(jnp.bfloat16)


def draw_rewards(key, part):
    position = jnp.arange(TOKENS, dtype=jnp.float32) / TOKENS
    member = jnp.arange(MICRO, dtype=jnp.float32) / MICRO
    scale = 1.0 + position[None, :] + member[:, None]
    noise = jnp.clip(jax.random.normal(jax.random.fold_in(key, 22), (MICRO, TOKENS), jnp.float32), -4.0, 4.0)
    return (noise * scale).astype(jnp.float32)


def shard_levels(own_key, extent, shards, least, top_value):
    factor_of = 1.0
    for dim, shards_of in shards:
        draws = jax.random.uniform(jax.random.fold_in(jax.random.fold_in(own_key, 6), dim), (shards_of,), jnp.float32, least / len(shards), top_value / len(shards))
        factor_of = factor_of * jnp.repeat(jnp.exp(draws), extent[dim] // shards_of).reshape((-1,) + (1,) * (len(extent) - 1 - dim))
    return factor_of


def length_profile(count, total, limit, skew):
    weights = [(1 << 20) // math.isqrt(rank ** skew) + 1 for rank in range(2, count + 1)]
    surplus, counts = total - limit - (count - 1), [1] * (count - 1)
    while surplus > 0:
        free = [i for i in range(count - 1) if counts[i] < limit]
        whole, left = sum([weights[i] for i in free]), surplus
        for i in free:
            more = min(limit - counts[i], max(1, left * weights[i] // whole), surplus)
            counts[i] = counts[i] + more
            surplus = surplus - more
    return np.array([limit] + counts)


def uneven(own_key, number_of, total, limit, lean):
    if number_of == 2:
        one = jax.random.randint(own_key, (), max(1, total - limit), min(limit, total - 1) + 1)
        return jnp.stack([one, total - one])
    lengths = jnp.asarray(length_profile(number_of, total, limit, lean), jnp.int32)
    couples = (number_of - 1) // 2
    giver, receiver = lengths[1:1 + 2 * couples:2], lengths[2:2 + 2 * couples:2]
    slack = jnp.minimum(giver - 1, limit - receiver)
    passed = jax.random.randint(jax.random.fold_in(own_key, 1), (couples,), 0, 1 << 20) % (slack + 1)
    lengths = lengths.at[1:1 + 2 * couples:2].set(giver - passed).at[2:2 + 2 * couples:2].set(receiver + passed)
    return lengths[jax.random.permutation(jax.random.fold_in(own_key, 2), number_of)]


def normal_values(rng, extent, scale, reach, pieces=(), held_as=jnp.bfloat16):
    gain = shard_levels(rng, extent, pieces, -0.22, 0.18) if pieces else 1.0
    values = jax.random.normal(rng, extent, jnp.float32) * scale * gain
    return jnp.minimum(jnp.maximum(values, -reach), reach).astype(held_as)


def setup_inputs(seed: int = 0) -> dict:
    keys = jax.random.split(jax.random.key(seed), 7)
    queries = draw_queries(jax.random.fold_in(keys[6], 71), 0)
    key_rows = draw_key_rows(jax.random.fold_in(keys[6], 71), 0)
    value_rows = normal_values(keys[2], (MICRO, TOKENS, FEAT), 1.0, 6.0, ((0, 8), (1, 4)))
    doc_ids = jax.vmap(lambda own: jnp.searchsorted(jnp.cumsum(uneven(own, 4 * N_TP, TOKENS, TOK_DEV // 2, 2)), jnp.arange(TOKENS), side="right"))(jax.random.split(keys[3], MICRO)).reshape((MICRO, TOKENS)).astype(jnp.int32)
    rewards = draw_rewards(jax.random.fold_in(keys[6], 71), 0)
    value_head = normal_values(keys[5], (FEAT,), (FEAT // 16) ** -0.5, 0.375, (), jnp.float32)
    return {"queries": queries, "key_rows": key_rows, "value_rows": value_rows, "doc_ids": doc_ids, "rewards": rewards, "value_head": value_head}


gae_decay = 0.95
epsilon = 1e-05

def attend_block(index, queries, key_pad, value_pad, doc_pad):
    blocks = TOKENS // TOK_DEV
    micro = index // blocks
    first = index % blocks * TOK_DEV
    zero = jnp.zeros((), jnp.int32)
    query_block = lax.dynamic_slice(queries, (micro, first, zero), (1, TOK_DEV, FEAT))[0]
    query_block = query_block.astype(jnp.float32).reshape(TOK_DEV, HEADS, HEAD)
    key_block = lax.dynamic_slice(key_pad, (micro, first, zero), (1, 2 * TOK_DEV, FEAT))[0]
    key_block = key_block.astype(jnp.float32).reshape(2 * TOK_DEV, HEADS, HEAD)
    value_block = lax.dynamic_slice(value_pad, (micro, first, zero), (1, 2 * TOK_DEV, FEAT))[0]
    value_block = value_block.astype(jnp.float32).reshape(2 * TOK_DEV, HEADS, HEAD)
    doc_block = lax.dynamic_slice(doc_pad, (micro, first), (1, 2 * TOK_DEV))[0]
    query_doc = doc_block[TOK_DEV:]
    key_pos = first - TOK_DEV + jnp.arange(2 * TOK_DEV, dtype=jnp.int32)
    query_pos = first + jnp.arange(TOK_DEV, dtype=jnp.int32)
    allowed = (key_pos[None, :] <= query_pos[:, None]) & (doc_block[None, :] == query_doc[:, None])
    scores = jnp.einsum('qhd,khd->hqk', query_block, key_block, precision=lax.Precision.HIGHEST) * HEAD ** (-0.5)
    scores = jnp.where(allowed[None], scores, jnp.float32(-1e+30))
    top = lax.optimization_barrier(jnp.max(scores, axis=-1, keepdims=True))
    expo = jnp.where(allowed[None], jnp.exp(scores - top), jnp.float32(0.0))
    total = lax.optimization_barrier(jnp.sum(expo, axis=-1))
    weights = lax.optimization_barrier(expo.astype(jnp.bfloat16)).astype(jnp.float32)
    output = jnp.einsum('hqk,khd->qhd', weights, value_block, precision=lax.Precision.HIGHEST)
    output = output / jnp.transpose(total)[:, :, None]
    return output.astype(jnp.bfloat16).reshape(TOK_DEV, FEAT)

def reference(queries, key_rows, value_rows, doc_ids, rewards, value_head):
    key_pad = jnp.pad(key_rows, ((0, 0), (TOK_DEV, 0), (0, 0)))
    value_pad = jnp.pad(value_rows, ((0, 0), (TOK_DEV, 0), (0, 0)))
    doc_pad = jnp.concatenate([jnp.full((MICRO, TOK_DEV), -1, jnp.int32), doc_ids.astype(jnp.int32)], axis=1)
    worker = partial(attend_block, queries=queries, key_pad=key_pad, value_pad=value_pad, doc_pad=doc_pad)
    indices = jnp.arange(MICRO * (TOKENS // TOK_DEV), dtype=jnp.int32)
    attended = lax.map(worker, indices).reshape(MICRO, TOKENS, FEAT)
    state = jnp.einsum('btf,f->bt', attended.astype(jnp.float32), value_head, precision=lax.Precision.HIGHEST)
    linked = jnp.concatenate([doc_ids[:, 1:] == doc_ids[:, :-1], jnp.zeros((MICRO, 1), bool)], axis=1)
    state_next = jnp.concatenate([state[:, 1:], jnp.zeros((MICRO, 1), jnp.float32)], axis=1)
    delta = rewards + jnp.where(linked, state_next, jnp.float32(0.0)) - state

    def advance(carry, inputs):
        delta_now, linked_now = inputs
        result = delta_now + gae_decay * jnp.where(linked_now, carry, jnp.float32(0.0))
        return (result, result)
    final_carry, gae = lax.scan(advance, jnp.zeros((MICRO,), jnp.float32), (jnp.transpose(delta), jnp.transpose(linked)), reverse=True)
    gae = jnp.transpose(gae)
    number = MICRO * TOKENS
    mean = jnp.sum(gae) / number
    spread = jnp.sum(gae * gae) / number - mean * mean
    advantages = (gae - mean) / jnp.sqrt(spread + epsilon)
    return (attended, advantages)
```

```python
import functools
import math

import jax
import jax.numpy as jnp
from jax import lax
from jax.experimental import pallas as pl
from jax.experimental.pallas import tpu as pltpu
from jax.sharding import PartitionSpec as P

HEAD = 128
GROUP = 8

gae_decay = 0.95
epsilon = 1e-05

MESH = pl.DeviceIdType.MESH
F32 = jnp.float32


def kernel(n_sec, n_tp, q_hbm, k_hbm, v_hbm, doc_ref, rew_ref, head_ref, out_hbm, adv_ref,
           qbuf, kbuf, vbuf, obuf, acc, tp_slot, sec_slot,
           load_sem, store_sem, ksend, krecv, vsend, vrecv,
           tp_send, tp_recv, sec_send, sec_recv):
    rows = qbuf.shape[0]
    feat = qbuf.shape[1]
    half = rows // 2
    width = GROUP * HEAD
    chunks = feat // width
    sec = lax.axis_index("sec")
    tp = lax.axis_index("tp")

    loads = [
        pltpu.make_async_copy(q_hbm.at[0], qbuf, load_sem.at[0]),
        pltpu.make_async_copy(k_hbm.at[0], kbuf.at[pl.ds(half, rows)], load_sem.at[1]),
        pltpu.make_async_copy(v_hbm.at[0], vbuf.at[pl.ds(half, rows)], load_sem.at[2]),
    ]
    for load in loads:
        load.start()

    barrier = pltpu.get_barrier_semaphore()
    for d in range(1, n_tp):
        pl.semaphore_signal(barrier, inc=1, device_id={"tp": lax.rem(tp + d, n_tp)}, device_id_type=MESH)
    for d in range(1, n_sec):
        pl.semaphore_signal(barrier, inc=1, device_id={"sec": lax.rem(sec + d, n_sec)}, device_id_type=MESH)
    pl.semaphore_wait(barrier, n_tp + n_sec - 2)

    def exchange(c):
        cols = pl.ds(c * width, width)
        nxt = {"tp": lax.rem(tp + 1, n_tp)}
        return (
            pltpu.make_async_remote_copy(
                src_ref=k_hbm.at[0, pl.ds(half, half), cols], dst_ref=kbuf.at[pl.ds(0, half), cols],
                send_sem=ksend.at[c], recv_sem=krecv.at[c], device_id=nxt, device_id_type=MESH),
            pltpu.make_async_remote_copy(
                src_ref=v_hbm.at[0, pl.ds(half, half), cols], dst_ref=vbuf.at[pl.ds(0, half), cols],
                send_sem=vsend.at[c], recv_sem=vrecv.at[c], device_id=nxt, device_id_type=MESH),
        )

    @pl.when(tp < n_tp - 1)
    def _():
        for c in range(chunks):
            for copy in exchange(c):
                copy.start()

    @pl.when(tp == 0)
    def _():
        kbuf[pl.ds(0, half), :] = jnp.zeros((half, feat), kbuf.dtype)
        vbuf[pl.ds(0, half), :] = jnp.zeros((half, feat), vbuf.dtype)

    start = pl.multiple_of(tp * rows, rows)
    prev = pl.multiple_of(jnp.maximum(tp - 1, 0) * rows, rows)
    after = pl.multiple_of(jnp.minimum(tp + 1, n_tp - 1) * rows, rows)
    doc_row = doc_ref[0:1, pl.ds(start, rows)].astype(F32)
    doc_prev = doc_ref[0:1, pl.ds(prev, rows)].astype(F32)
    doc_next = doc_ref[0:1, pl.ds(after, rows)].astype(F32)[:, 0:1]
    doc_prev = jnp.where(tp > 0, doc_prev, jnp.float32(-1.0))
    doc_key = jnp.broadcast_to(doc_row, (rows, rows))
    doc_query = doc_key.T
    row_id = lax.broadcasted_iota(jnp.int32, (rows, rows), 0)
    col_id = lax.broadcasted_iota(jnp.int32, (rows, rows), 1)
    same = (col_id <= row_id) & (doc_key == doc_query)
    decay_log = math.log(gae_decay)
    table = jnp.where(same, jnp.exp((row_id - col_id).astype(F32) * decay_log), F32(0.0))
    lane = lax.broadcasted_iota(jnp.int32, (half, rows), 1)
    line = lax.broadcasted_iota(jnp.int32, (half, rows), 0)
    key_lo = jnp.broadcast_to(
        jnp.where(lane[0:1] < half, pltpu.roll(doc_prev, half, 1), pltpu.roll(doc_row, half, 1)), (half, rows))
    allowed_lo = (lane - half <= line) & (key_lo == doc_query[0:half])
    allowed_hi = (lane <= line + half) & (doc_key[half:] == doc_query[half:])

    scale = HEAD ** (-0.5)

    def attend(c, first, key_first, allowed):
        total_state = jnp.zeros((half, HEAD), F32)
        spans = [pl.ds(pl.multiple_of(c * width + g * HEAD, HEAD), HEAD) for g in range(GROUP)]
        expos = []
        for g in range(GROUP):
            raw = lax.dot_general(
                qbuf[pl.ds(first, half), spans[g]], kbuf[pl.ds(key_first, rows), spans[g]],
                (((1,), (1,)), ((), ())), preferred_element_type=F32)
            expos.append(jnp.where(allowed, raw * scale, F32(-1e30)))
        for g in range(GROUP):
            top = jnp.max(expos[g], axis=-1, keepdims=True)
            expo = jnp.exp(expos[g] - top)
            total = jnp.sum(expo, axis=-1, keepdims=True)
            summed = jnp.dot(expo.astype(jnp.bfloat16), vbuf[pl.ds(key_first, rows), spans[g]],
                             preferred_element_type=F32)
            result = (summed / total).astype(jnp.bfloat16)
            obuf[pl.ds(first, half), spans[g]] = result
            total_state = total_state + result.astype(F32) * head_ref[0:1, spans[g]]
        return total_state

    for load in loads:
        load.wait()

    acc_hi = lax.fori_loop(
        0, chunks, lambda c, held: held + attend(c, half, half, allowed_hi), jnp.zeros((half, HEAD), F32))
    acc[pl.ds(half, half), :] = acc_hi
    store_hi = pltpu.make_async_copy(
        obuf.at[pl.ds(half, half)], out_hbm.at[0, pl.ds(half, half)], store_sem.at[0])
    store_hi.start()

    acc_lo = jnp.zeros((half, HEAD), F32)
    stores = [store_hi]
    for c in range(chunks):
        @pl.when(tp > 0)
        def _():
            for copy in exchange(c):
                copy.wait_recv()
        acc_lo = acc_lo + attend(c, 0, 0, allowed_lo)
    store_lo = pltpu.make_async_copy(
        obuf.at[pl.ds(0, half)], out_hbm.at[0, pl.ds(0, half)], store_sem.at[1])
    store_lo.start()
    stores.append(store_lo)
    acc[pl.ds(0, half), :] = acc_lo

    state = jnp.sum(acc[...].T, axis=0, keepdims=True)
    spot = lax.broadcasted_iota(jnp.int32, (1, rows), 1)
    linked = (pltpu.roll(doc_row, rows - 1, 1) == doc_row) & (spot < rows - 1)
    delta = rew_ref[...] + jnp.where(linked, pltpu.roll(state, rows - 1, 1), F32(0.0)) - state
    gae_local = jnp.sum(table * jnp.broadcast_to(delta, (rows, rows)).T, axis=0, keepdims=True)
    joined = (doc_row == doc_next) & (tp < n_tp - 1)
    coef = jnp.where(joined, jnp.exp((rows - 1 - spot).astype(F32) * decay_log), F32(0.0))
    carry = state[:, 0:1] + gae_decay * gae_local[:, 0:1]

    def summed(x):
        return jnp.broadcast_to(jnp.sum(x, axis=1, keepdims=True), (1, rows))

    rows_out = [summed(gae_local), summed(gae_local * gae_local), summed(coef),
                summed(coef * gae_local), summed(coef * coef), jnp.broadcast_to(carry, (1, rows))]
    for i, value in enumerate(rows_out):
        tp_slot[tp, pl.ds(i, 1), :] = value

    def tp_copy(d):
        return pltpu.make_async_remote_copy(
            src_ref=tp_slot.at[tp], dst_ref=tp_slot.at[tp], send_sem=tp_send.at[d], recv_sem=tp_recv.at[tp],
            device_id={"tp": lax.rem(tp + d, n_tp)}, device_id_type=MESH)

    def tp_wait(peer):
        return pltpu.make_async_remote_copy(
            src_ref=tp_slot.at[peer], dst_ref=tp_slot.at[peer], send_sem=tp_send.at[0], recv_sem=tp_recv.at[peer],
            device_id={"tp": peer}, device_id_type=MESH)

    for d in range(1, n_tp):
        tp_copy(d).start()
    for d in range(1, n_tp):
        tp_wait(lax.rem(tp + d, n_tp)).wait_recv()

    mean_part = jnp.zeros((1, rows), F32)
    square_part = jnp.zeros((1, rows), F32)
    mine = jnp.zeros((1, rows), F32)
    for t in range(n_tp):
        part = tp_slot[t]
        arrived = tp_slot[t + 1][5:6] if t + 1 < n_tp else jnp.zeros((1, rows), F32)
        mean_part = mean_part + part[0:1] + part[2:3] * arrived
        square_part = square_part + part[1:2] + 2.0 * part[3:4] * arrived + part[4:5] * arrived * arrived
        mine = jnp.where(tp == t, arrived, mine)
    gae = gae_local + coef * mine

    sec_slot[sec, pl.ds(0, 1), :] = mean_part
    sec_slot[sec, pl.ds(1, 1), :] = square_part

    def sec_copy(d):
        return pltpu.make_async_remote_copy(
            src_ref=sec_slot.at[sec], dst_ref=sec_slot.at[sec], send_sem=sec_send.at[d], recv_sem=sec_recv.at[sec],
            device_id={"sec": lax.rem(sec + d, n_sec)}, device_id_type=MESH)

    def sec_wait(peer):
        return pltpu.make_async_remote_copy(
            src_ref=sec_slot.at[peer], dst_ref=sec_slot.at[peer], send_sem=sec_send.at[0],
            recv_sem=sec_recv.at[peer], device_id={"sec": peer}, device_id_type=MESH)

    for d in range(1, n_sec):
        sec_copy(d).start()
    for d in range(1, n_sec):
        sec_wait(lax.rem(sec + d, n_sec)).wait_recv()

    total_sum = jnp.zeros((1, rows), F32)
    square_sum = jnp.zeros((1, rows), F32)
    for s in range(n_sec):
        part = sec_slot[s]
        total_sum = total_sum + part[0:1]
        square_sum = square_sum + part[1:2]
    number = n_sec * n_tp * rows
    mean = total_sum / number
    spread = square_sum / number - mean * mean
    adv_ref[...] = (gae - mean) / jnp.sqrt(spread + epsilon)

    for store in stores:
        store.wait()
    for d in range(1, n_tp):
        tp_copy(d).wait_send()
    for d in range(1, n_sec):
        sec_copy(d).wait_send()

    @pl.when(tp < n_tp - 1)
    def _():
        for c in range(chunks):
            for copy in exchange(c):
                copy.wait_send()


def local(n_sec, n_tp, queries, key_rows, value_rows, doc_ids, rewards, value_head):
    rows, feat = queries.shape[1:]
    half = rows // 2
    chunks = feat // (GROUP * HEAD)
    any_spec = pl.BlockSpec(memory_space=pl.ANY)
    vmem_spec = pl.BlockSpec(memory_space=pltpu.VMEM)
    dma = pltpu.SemaphoreType.DMA
    bf16 = jnp.bfloat16
    return pl.pallas_call(
        functools.partial(kernel, n_sec, n_tp),
        out_shape=(jax.ShapeDtypeStruct((1, rows, feat), bf16), jax.ShapeDtypeStruct((1, rows), F32)),
        in_specs=[any_spec, any_spec, any_spec, vmem_spec, vmem_spec, vmem_spec],
        out_specs=(any_spec, vmem_spec),
        scratch_shapes=[
            pltpu.VMEM((rows, feat), bf16),
            pltpu.VMEM((rows + half, feat), bf16),
            pltpu.VMEM((rows + half, feat), bf16),
            pltpu.VMEM((rows, feat), bf16),
            pltpu.VMEM((rows, HEAD), F32),
            pltpu.VMEM((n_tp, 8, rows), F32),
            pltpu.VMEM((n_sec, 8, rows), F32),
            dma((3,)), dma((2,)),
            dma((chunks,)), dma((chunks,)), dma((chunks,)), dma((chunks,)),
            dma((n_tp,)), dma((n_tp,)), dma((n_sec,)), dma((n_sec,)),
        ],
        compiler_params=pltpu.CompilerParams(collective_id=0, has_side_effects=True),
    )(queries, key_rows, value_rows, doc_ids, rewards, value_head.reshape(1, feat))


def solution(mesh):
    return jax.shard_map(
        functools.partial(local, mesh.shape["sec"], mesh.shape["tp"]),
        mesh=mesh,
        in_specs=(
            P("sec", "tp", None),
            P("sec", "tp", None),
            P("sec", "tp", None),
            P("sec", None),
            P("sec", "tp"),
            P(),
        ),
        out_specs=(P("sec", "tp", None), P("sec", "tp")),
        check_vma=False,
    )
```

```python
import functools
import math

import jax
import jax.numpy as jnp
from jax import lax
from jax.experimental import pallas as pl
from jax.experimental.pallas import tpu as pltpu
from jax.sharding import PartitionSpec as P

HEAD = 128
GROUP = 8

gae_decay = 0.95
epsilon = 1e-05

MESH = pl.DeviceIdType.MESH
F32 = jnp.float32


def kernel(n_sec, n_tp, q_hbm, k_hbm, v_hbm, doc_ref, rew_ref, head_ref, out_hbm, adv_ref,
           qbuf, kbuf, vbuf, obuf, q_in, mixed, lse_out, lse_in, acc, tp_slot, sec_slot,
           load_sem, store_sem, qsend, qrecv, ksend, krecv, vsend, vrecv, lsend, lrecv,
           tp_send, tp_recv, sec_send, sec_recv):
    rows = qbuf.shape[0]
    feat = qbuf.shape[1]
    half = rows // 2
    part = half // 2
    width = GROUP * HEAD
    chunks = feat // width
    sec = lax.axis_index("sec")
    tp = lax.axis_index("tp")

    loads = [
        pltpu.make_async_copy(q_hbm.at[0], qbuf, load_sem.at[0]),
        pltpu.make_async_copy(k_hbm.at[0], kbuf.at[pl.ds(part, rows)], load_sem.at[1]),
        pltpu.make_async_copy(v_hbm.at[0], vbuf.at[pl.ds(part, rows)], load_sem.at[2]),
    ]
    for load in loads:
        load.start()

    barrier = pltpu.get_barrier_semaphore()
    for d in range(1, n_tp):
        pl.semaphore_signal(barrier, inc=1, device_id={"tp": lax.rem(tp + d, n_tp)}, device_id_type=MESH)
    for d in range(1, n_sec):
        pl.semaphore_signal(barrier, inc=1, device_id={"sec": lax.rem(sec + d, n_sec)}, device_id_type=MESH)
    pl.semaphore_wait(barrier, n_tp + n_sec - 2)

    following = {"tp": lax.rem(tp + 1, n_tp)}
    preceding = {"tp": lax.rem(tp + n_tp - 1, n_tp)}

    def columns(c):
        return pl.ds(pl.multiple_of(c * width, width), width)

    def send_queries(c):
        return pltpu.make_async_remote_copy(
            src_ref=q_hbm.at[0, pl.ds(0, part), columns(c)], dst_ref=q_in.at[:, columns(c)],
            send_sem=qsend.at[c], recv_sem=qrecv.at[c], device_id=preceding, device_id_type=MESH)

    def send_keys(c):
        return pltpu.make_async_remote_copy(
            src_ref=k_hbm.at[0, pl.ds(rows - part, part), columns(c)], dst_ref=kbuf.at[pl.ds(0, part), columns(c)],
            send_sem=ksend.at[c], recv_sem=krecv.at[c], device_id=following, device_id_type=MESH)

    def send_mixed(c):
        return pltpu.make_async_remote_copy(
            src_ref=mixed.at[:, columns(c)], dst_ref=vbuf.at[pl.ds(0, part), columns(c)],
            send_sem=vsend.at[c], recv_sem=vrecv.at[c], device_id=following, device_id_type=MESH)

    def send_lse():
        return pltpu.make_async_remote_copy(
            src_ref=lse_out, dst_ref=lse_in, send_sem=lsend, recv_sem=lrecv,
            device_id=following, device_id_type=MESH)

    sends_on = tp < n_tp - 1
    receives = tp > 0

    @pl.when(receives)
    def _():
        for c in range(chunks):
            send_queries(c).start()

    @pl.when(sends_on)
    def _():
        for c in range(chunks):
            send_keys(c).start()

    @pl.when(tp == 0)
    def _():
        kbuf[pl.ds(0, part), :] = jnp.zeros((part, feat), kbuf.dtype)
        vbuf[pl.ds(0, part), :] = jnp.zeros((part, feat), vbuf.dtype)
        lse_in[...] = jnp.zeros(lse_in.shape, F32)

    lse_out[...] = jnp.zeros(lse_out.shape, F32)

    start = pl.multiple_of(tp * rows, rows)
    prev = pl.multiple_of(jnp.maximum(tp - 1, 0) * rows, rows)
    after = pl.multiple_of(jnp.minimum(tp + 1, n_tp - 1) * rows, rows)
    doc_row = doc_ref[0:1, pl.ds(start, rows)].astype(F32)
    doc_prev = doc_ref[0:1, pl.ds(prev, rows)].astype(F32)
    doc_next = doc_ref[0:1, pl.ds(after, rows)].astype(F32)[:, 0:1]
    doc_prev = jnp.where(tp > 0, doc_prev, jnp.float32(-1.0))
    doc_key = jnp.broadcast_to(doc_row, (rows, rows))
    doc_query = doc_key.T
    row_id = lax.broadcasted_iota(jnp.int32, (rows, rows), 0)
    col_id = lax.broadcasted_iota(jnp.int32, (rows, rows), 1)
    same = (col_id <= row_id) & (doc_key == doc_query)
    decay_log = math.log(gae_decay)
    table = jnp.where(same, jnp.exp((row_id - col_id).astype(F32) * decay_log), F32(0.0))
    before = jnp.sum(jnp.where(doc_prev == doc_row[:, 0:1], F32(1.0), F32(0.0)), axis=1, keepdims=True)
    before_next = jnp.sum(jnp.where(doc_row == doc_next, F32(1.0), F32(0.0)), axis=1, keepdims=True)
    given = before > part
    giving = before_next > part
    given_rows = given & (doc_query[0:part, 0:1] == doc_prev[:, rows - 1 : rows])
    doc_keys_prev = jnp.where(given, F32(-1.0), doc_prev)
    lane = lax.broadcasted_iota(jnp.int32, (half, rows), 1)
    line = lax.broadcasted_iota(jnp.int32, (half, rows), 0)
    key_lo = jnp.broadcast_to(
        jnp.where(lane[0:1] < part, pltpu.roll(doc_keys_prev, part, 1), pltpu.roll(doc_row, part, 1)), (half, rows))
    allowed_lo = (lane - part <= line) & (key_lo == doc_query[0:half])
    allowed_hi = (lane <= line + half) & (doc_key[half:] == doc_query[half:])
    allowed_next = jnp.broadcast_to(doc_row == doc_next, (part, rows)) & (lane[0:part] >= half)
    giving_all = jnp.broadcast_to(giving, (part, HEAD))
    head_lane = lax.broadcasted_iota(jnp.int32, (part, HEAD), 1)

    scale = HEAD ** (-0.5)

    def spans_of(c):
        return [pl.ds(pl.multiple_of(c * width + g * HEAD, HEAD), HEAD) for g in range(GROUP)]

    def scores(query, key, allowed):
        raw = lax.dot_general(query, key, (((1,), (1,)), ((), ())), preferred_element_type=F32)
        return jnp.where(allowed, raw * scale, F32(-1e30))

    def attend_hi(c):
        spans = spans_of(c)
        total_state = jnp.zeros((half, HEAD), F32)
        found = [scores(qbuf[pl.ds(half, half), s], kbuf[pl.ds(part, rows), s], allowed_hi) for s in spans]
        for g, s in enumerate(spans):
            top = jnp.max(found[g], axis=-1, keepdims=True)
            expo = jnp.exp(found[g] - top)
            total = jnp.sum(expo, axis=-1, keepdims=True)
            added = jnp.dot(expo.astype(jnp.bfloat16), vbuf[pl.ds(part, rows), s], preferred_element_type=F32)
            result = (added / total).astype(jnp.bfloat16)
            obuf[pl.ds(half, half), s] = result
            total_state = total_state + result.astype(F32) * head_ref[0:1, s]
        return total_state

    def attend_next(c):
        spans = spans_of(c)
        found = [scores(q_in[:, s], kbuf[pl.ds(part, rows), s], allowed_next) for s in spans]
        sums = lse_out[...]
        for g, s in enumerate(spans):
            top = jnp.max(found[g], axis=-1, keepdims=True)
            expo = jnp.exp(found[g] - top)
            total = jnp.sum(expo, axis=-1, keepdims=True)
            added = jnp.dot(expo.astype(jnp.bfloat16), vbuf[pl.ds(part, rows), s], preferred_element_type=F32)
            own = vbuf[pl.ds(rows, part), s]
            mixed[:, s] = jnp.where(giving_all, added / total, own.astype(F32)).astype(jnp.bfloat16)
            sums = jnp.where(head_lane == c * GROUP + g, top + jnp.log(total), sums)
        lse_out[...] = sums

    def attend_lo(c):
        spans = spans_of(c)
        total_state = jnp.zeros((half, HEAD), F32)
        found = [scores(qbuf[pl.ds(0, half), s], kbuf[pl.ds(0, rows), s], allowed_lo) for s in spans]
        for g, s in enumerate(spans):
            h = c * GROUP + g
            other = jnp.where(given_rows, lse_in[:, h : h + 1], F32(-1e30))
            top = jnp.max(found[g], axis=-1, keepdims=True)
            top = jnp.concatenate([jnp.maximum(top[0:part], other), top[part:]], axis=0)
            expo = jnp.exp(found[g] - top)
            total = jnp.sum(expo, axis=-1, keepdims=True)
            added = jnp.dot(expo.astype(jnp.bfloat16), vbuf[pl.ds(0, rows), s], preferred_element_type=F32)
            share = jnp.exp(other - top[0:part])
            first = (added[0:part] + share * vbuf[pl.ds(0, part), s].astype(F32)) / (total[0:part] + share)
            result = jnp.concatenate([first, added[part:] / total[part:]], axis=0).astype(jnp.bfloat16)
            obuf[pl.ds(0, half), s] = result
            total_state = total_state + result.astype(F32) * head_ref[0:1, s]
        return total_state

    for load in loads:
        load.wait()

    def first_phase(c, held):
        held = held + attend_hi(c)

        @pl.when(sends_on)
        def _():
            send_queries(c).wait_recv()
            attend_next(c)
            send_mixed(c).start()

        return held

    acc[pl.ds(half, half), :] = lax.fori_loop(0, chunks, first_phase, jnp.zeros((half, HEAD), F32))

    @pl.when(sends_on)
    def _():
        send_lse().start()

    store_hi = pltpu.make_async_copy(
        obuf.at[pl.ds(half, half)], out_hbm.at[0, pl.ds(half, half)], store_sem.at[0])
    store_hi.start()

    @pl.when(receives)
    def _():
        send_lse().wait_recv()

    acc_lo = jnp.zeros((half, HEAD), F32)
    for c in range(chunks):
        @pl.when(receives)
        def _():
            send_keys(c).wait_recv()
            send_mixed(c).wait_recv()
        acc_lo = acc_lo + attend_lo(c)
    acc[pl.ds(0, half), :] = acc_lo
    store_lo = pltpu.make_async_copy(
        obuf.at[pl.ds(0, half)], out_hbm.at[0, pl.ds(0, half)], store_sem.at[1])
    store_lo.start()
    stores = [store_hi, store_lo]

    state = jnp.sum(acc[...].T, axis=0, keepdims=True)
    spot = lax.broadcasted_iota(jnp.int32, (1, rows), 1)
    linked = (pltpu.roll(doc_row, rows - 1, 1) == doc_row) & (spot < rows - 1)
    delta = rew_ref[...] + jnp.where(linked, pltpu.roll(state, rows - 1, 1), F32(0.0)) - state
    gae_local = jnp.sum(table * jnp.broadcast_to(delta, (rows, rows)).T, axis=0, keepdims=True)
    joined = (doc_row == doc_next) & (tp < n_tp - 1)
    coef = jnp.where(joined, jnp.exp((rows - 1 - spot).astype(F32) * decay_log), F32(0.0))
    carry = state[:, 0:1] + gae_decay * gae_local[:, 0:1]

    def summed(x):
        return jnp.broadcast_to(jnp.sum(x, axis=1, keepdims=True), (1, rows))

    rows_out = [summed(gae_local), summed(gae_local * gae_local), summed(coef),
                summed(coef * gae_local), summed(coef * coef), jnp.broadcast_to(carry, (1, rows))]
    for i, value in enumerate(rows_out):
        tp_slot[tp, pl.ds(i, 1), :] = value

    def tp_copy(d):
        return pltpu.make_async_remote_copy(
            src_ref=tp_slot.at[tp], dst_ref=tp_slot.at[tp], send_sem=tp_send.at[d], recv_sem=tp_recv.at[tp],
            device_id={"tp": lax.rem(tp + d, n_tp)}, device_id_type=MESH)

    def tp_wait(peer):
        return pltpu.make_async_remote_copy(
            src_ref=tp_slot.at[peer], dst_ref=tp_slot.at[peer], send_sem=tp_send.at[0], recv_sem=tp_recv.at[peer],
            device_id={"tp": peer}, device_id_type=MESH)

    for d in range(1, n_tp):
        tp_copy(d).start()
    for d in range(1, n_tp):
        tp_wait(lax.rem(tp + d, n_tp)).wait_recv()

    mean_part = jnp.zeros((1, rows), F32)
    square_part = jnp.zeros((1, rows), F32)
    mine = jnp.zeros((1, rows), F32)
    for t in range(n_tp):
        held = tp_slot[t]
        arrived = tp_slot[t + 1][5:6] if t + 1 < n_tp else jnp.zeros((1, rows), F32)
        mean_part = mean_part + held[0:1] + held[2:3] * arrived
        square_part = square_part + held[1:2] + 2.0 * held[3:4] * arrived + held[4:5] * arrived * arrived
        mine = jnp.where(tp == t, arrived, mine)
    gae = gae_local + coef * mine

    sec_slot[sec, pl.ds(0, 1), :] = mean_part
    sec_slot[sec, pl.ds(1, 1), :] = square_part

    def sec_copy(d):
        return pltpu.make_async_remote_copy(
            src_ref=sec_slot.at[sec], dst_ref=sec_slot.at[sec], send_sem=sec_send.at[d], recv_sem=sec_recv.at[sec],
            device_id={"sec": lax.rem(sec + d, n_sec)}, device_id_type=MESH)

    def sec_wait(peer):
        return pltpu.make_async_remote_copy(
            src_ref=sec_slot.at[peer], dst_ref=sec_slot.at[peer], send_sem=sec_send.at[0],
            recv_sem=sec_recv.at[peer], device_id={"sec": peer}, device_id_type=MESH)

    for d in range(1, n_sec):
        sec_copy(d).start()
    for d in range(1, n_sec):
        sec_wait(lax.rem(sec + d, n_sec)).wait_recv()

    total_sum = jnp.zeros((1, rows), F32)
    square_sum = jnp.zeros((1, rows), F32)
    for s in range(n_sec):
        held = sec_slot[s]
        total_sum = total_sum + held[0:1]
        square_sum = square_sum + held[1:2]
    number = n_sec * n_tp * rows
    mean = total_sum / number
    spread = square_sum / number - mean * mean
    adv_ref[...] = (gae - mean) / jnp.sqrt(spread + epsilon)

    for store in stores:
        store.wait()
    for d in range(1, n_tp):
        tp_copy(d).wait_send()
    for d in range(1, n_sec):
        sec_copy(d).wait_send()

    @pl.when(receives)
    def _():
        for c in range(chunks):
            send_queries(c).wait_send()

    @pl.when(sends_on)
    def _():
        for c in range(chunks):
            send_keys(c).wait_send()
            send_mixed(c).wait_send()
        send_lse().wait_send()


def local(n_sec, n_tp, queries, key_rows, value_rows, doc_ids, rewards, value_head):
    rows, feat = queries.shape[1:]
    part = rows // 4
    chunks = feat // (GROUP * HEAD)
    any_spec = pl.BlockSpec(memory_space=pl.ANY)
    vmem_spec = pl.BlockSpec(memory_space=pltpu.VMEM)
    dma = pltpu.SemaphoreType.DMA
    bf16 = jnp.bfloat16
    return pl.pallas_call(
        functools.partial(kernel, n_sec, n_tp),
        out_shape=(jax.ShapeDtypeStruct((1, rows, feat), bf16), jax.ShapeDtypeStruct((1, rows), F32)),
        in_specs=[any_spec, any_spec, any_spec, vmem_spec, vmem_spec, vmem_spec],
        out_specs=(any_spec, vmem_spec),
        scratch_shapes=[
            pltpu.VMEM((rows, feat), bf16),
            pltpu.VMEM((rows + part, feat), bf16),
            pltpu.VMEM((rows + part, feat), bf16),
            pltpu.VMEM((rows, feat), bf16),
            pltpu.VMEM((part, feat), bf16),
            pltpu.VMEM((part, feat), bf16),
            pltpu.VMEM((part, HEAD), F32),
            pltpu.VMEM((part, HEAD), F32),
            pltpu.VMEM((rows, HEAD), F32),
            pltpu.VMEM((n_tp, 8, rows), F32),
            pltpu.VMEM((n_sec, 8, rows), F32),
            dma((3,)), dma((2,)),
            dma((chunks,)), dma((chunks,)), dma((chunks,)), dma((chunks,)), dma((chunks,)), dma((chunks,)), dma, dma,
            dma((n_tp,)), dma((n_tp,)), dma((n_sec,)), dma((n_sec,)),
        ],
        compiler_params=pltpu.CompilerParams(collective_id=0, has_side_effects=True),
    )(queries, key_rows, value_rows, doc_ids, rewards, value_head.reshape(1, feat))


def solution(mesh):
    return jax.shard_map(
        functools.partial(local, mesh.shape["sec"], mesh.shape["tp"]),
        mesh=mesh,
        in_specs=(
            P("sec", "tp", None),
            P("sec", "tp", None),
            P("sec", "tp", None),
            P("sec", None),
            P("sec", "tp"),
            P(),
        ),
        out_specs=(P("sec", "tp", None), P("sec", "tp")),
        check_vma=False,
    )
```

```python
import functools
import math

import jax
import jax.numpy as jnp
from jax import lax
from jax.experimental import pallas as pl
from jax.experimental.pallas import tpu as pltpu
from jax.sharding import PartitionSpec as P

HEAD = 128
GROUP = 8

gae_decay = 0.95
epsilon = 1e-05

MESH = pl.DeviceIdType.MESH
F32 = jnp.float32


def kernel(n_sec, n_tp, q_hbm, k_hbm, v_hbm, doc_hbm, rew_hbm, head_hbm, out_hbm, adv_ref,
           obuf, doc_ref, rew_ref, head_ref, qbuf, kbuf, vbuf, q_in, mixed, lse_out, lse_in, acc, tp_slot, sec_slot,
           load_sem, store_sem, qsend, qrecv, ksend, krecv, vsend, vrecv, lsend, lrecv,
           tp_send, tp_recv, sec_send, sec_recv):
    rows = qbuf.shape[0]
    feat = qbuf.shape[1]
    half = rows // 2
    part = half // 2
    width = GROUP * HEAD
    chunks = feat // width
    sec = lax.axis_index("sec")
    tp = lax.axis_index("tp")

    barrier = pltpu.get_barrier_semaphore()
    for d in range(1, n_tp):
        pl.semaphore_signal(barrier, inc=1, device_id={"tp": lax.rem(tp + d, n_tp)}, device_id_type=MESH)
    for d in range(1, n_sec):
        pl.semaphore_signal(barrier, inc=1, device_id={"sec": lax.rem(sec + d, n_sec)}, device_id_type=MESH)
    small = [
        pltpu.make_async_copy(doc_hbm, doc_ref, load_sem.at[3]),
        pltpu.make_async_copy(rew_hbm, rew_ref, load_sem.at[4]),
        pltpu.make_async_copy(head_hbm, head_ref, load_sem.at[5]),
    ]
    loads = [
        pltpu.make_async_copy(q_hbm.at[0], qbuf, load_sem.at[0]),
        pltpu.make_async_copy(k_hbm.at[0], kbuf.at[pl.ds(part, rows)], load_sem.at[1]),
        pltpu.make_async_copy(v_hbm.at[0], vbuf.at[pl.ds(part, rows)], load_sem.at[2]),
    ]
    for load in small + loads:
        load.start()

    pl.semaphore_wait(barrier, n_tp + n_sec - 2)

    following = {"tp": lax.rem(tp + 1, n_tp)}
    preceding = {"tp": lax.rem(tp + n_tp - 1, n_tp)}

    def columns(c):
        return pl.ds(pl.multiple_of(c * width, width), width)

    def send_queries(c):
        return pltpu.make_async_remote_copy(
            src_ref=q_hbm.at[0, pl.ds(0, part), columns(c)], dst_ref=q_in.at[:, columns(c)],
            send_sem=qsend.at[c], recv_sem=qrecv.at[c], device_id=preceding, device_id_type=MESH)

    def send_keys(c):
        return pltpu.make_async_remote_copy(
            src_ref=k_hbm.at[0, pl.ds(rows - part, part), columns(c)], dst_ref=kbuf.at[pl.ds(0, part), columns(c)],
            send_sem=ksend.at[c], recv_sem=krecv.at[c], device_id=following, device_id_type=MESH)

    def send_mixed(c):
        return pltpu.make_async_remote_copy(
            src_ref=mixed.at[:, columns(c)], dst_ref=vbuf.at[pl.ds(0, part), columns(c)],
            send_sem=vsend.at[c], recv_sem=vrecv.at[c], device_id=following, device_id_type=MESH)

    def send_lse():
        return pltpu.make_async_remote_copy(
            src_ref=lse_out, dst_ref=lse_in, send_sem=lsend, recv_sem=lrecv,
            device_id=following, device_id_type=MESH)

    sends_on = tp < n_tp - 1
    receives = tp > 0

    @pl.when(receives)
    def _():
        for c in range(chunks):
            send_queries(c).start()

    @pl.when(sends_on)
    def _():
        for c in range(chunks):
            send_keys(c).start()

    @pl.when(tp == 0)
    def _():
        kbuf[pl.ds(0, part), :] = jnp.zeros((part, feat), kbuf.dtype)
        vbuf[pl.ds(0, part), :] = jnp.zeros((part, feat), vbuf.dtype)
        lse_in[...] = jnp.zeros(lse_in.shape, F32)

    lse_out[...] = jnp.zeros(lse_out.shape, F32)

    for load in small:
        load.wait()
    start = pl.multiple_of(tp * rows, rows)
    prev = pl.multiple_of(jnp.maximum(tp - 1, 0) * rows, rows)
    after = pl.multiple_of(jnp.minimum(tp + 1, n_tp - 1) * rows, rows)
    doc_row = doc_ref[0:1, pl.ds(start, rows)].astype(F32)
    doc_prev = doc_ref[0:1, pl.ds(prev, rows)].astype(F32)
    doc_next = doc_ref[0:1, pl.ds(after, rows)].astype(F32)[:, 0:1]
    doc_prev = jnp.where(tp > 0, doc_prev, jnp.float32(-1.0))
    doc_key = jnp.broadcast_to(doc_row, (rows, rows))
    doc_query = doc_key.T
    row_id = lax.broadcasted_iota(jnp.int32, (rows, rows), 0)
    col_id = lax.broadcasted_iota(jnp.int32, (rows, rows), 1)
    same = (col_id <= row_id) & (doc_key == doc_query)
    decay_log = math.log(gae_decay)
    table = jnp.where(same, jnp.exp((row_id - col_id).astype(F32) * decay_log), F32(0.0))
    before = jnp.sum(jnp.where(doc_prev == doc_row[:, 0:1], F32(1.0), F32(0.0)), axis=1, keepdims=True)
    before_next = jnp.sum(jnp.where(doc_row == doc_next, F32(1.0), F32(0.0)), axis=1, keepdims=True)
    given = before > part
    giving = before_next > part
    given_rows = given & (doc_query[0:part, 0:1] == doc_prev[:, rows - 1 : rows])
    doc_keys_prev = jnp.where(given, F32(-1.0), doc_prev)
    lane = lax.broadcasted_iota(jnp.int32, (half, rows), 1)
    line = lax.broadcasted_iota(jnp.int32, (half, rows), 0)
    key_lo = jnp.broadcast_to(
        jnp.where(lane[0:1] < part, pltpu.roll(doc_keys_prev, part, 1), pltpu.roll(doc_row, part, 1)), (half, rows))
    allowed_lo = (lane - part <= line) & (key_lo == doc_query[0:half])
    allowed_hi = (lane <= line + half) & (doc_key[half:] == doc_query[half:])
    allowed_next = jnp.broadcast_to(doc_row == doc_next, (part, rows)) & (lane[0:part] >= half)
    giving_all = jnp.broadcast_to(giving, (part, HEAD))
    head_lane = lax.broadcasted_iota(jnp.int32, (part, HEAD), 1)

    scale = HEAD ** (-0.5)

    def spans_of(c):
        return [pl.ds(pl.multiple_of(c * width + g * HEAD, HEAD), HEAD) for g in range(GROUP)]

    def scores(query, key, allowed):
        raw = lax.dot_general(query, key, (((1,), (1,)), ((), ())), preferred_element_type=F32)
        return jnp.where(allowed, raw * scale, F32(-1e30))

    def attend_hi(c):
        spans = spans_of(c)
        total_state = jnp.zeros((half, HEAD), F32)
        found = [scores(qbuf[pl.ds(half, half), s], kbuf[pl.ds(part, rows), s], allowed_hi) for s in spans]
        for g, s in enumerate(spans):
            top = jnp.max(found[g], axis=-1, keepdims=True)
            expo = jnp.exp(found[g] - top)
            total = jnp.sum(expo, axis=-1, keepdims=True)
            added = jnp.dot(expo.astype(jnp.bfloat16), vbuf[pl.ds(part, rows), s], preferred_element_type=F32)
            result = (added / total).astype(jnp.bfloat16)
            obuf[pl.ds(half, half), s] = result
            total_state = total_state + result.astype(F32) * head_ref[0:1, s]
        return total_state

    def attend_next(c):
        spans = spans_of(c)
        found = [scores(q_in[:, s], kbuf[pl.ds(part, rows), s], allowed_next) for s in spans]
        sums = lse_out[...]
        for g, s in enumerate(spans):
            top = jnp.max(found[g], axis=-1, keepdims=True)
            expo = jnp.exp(found[g] - top)
            total = jnp.sum(expo, axis=-1, keepdims=True)
            added = jnp.dot(expo.astype(jnp.bfloat16), vbuf[pl.ds(part, rows), s], preferred_element_type=F32)
            own = vbuf[pl.ds(rows, part), s]
            mixed[:, s] = jnp.where(giving_all, added / total, own.astype(F32)).astype(jnp.bfloat16)
            sums = jnp.where(head_lane == c * GROUP + g, top + jnp.log(total), sums)
        lse_out[...] = sums

    def attend_lo(c):
        spans = spans_of(c)
        total_state = jnp.zeros((half, HEAD), F32)
        found = [scores(qbuf[pl.ds(0, half), s], kbuf[pl.ds(0, rows), s], allowed_lo) for s in spans]
        for g, s in enumerate(spans):
            h = c * GROUP + g
            other = jnp.where(given_rows, lse_in[:, h : h + 1], F32(-1e30))
            top = jnp.max(found[g], axis=-1, keepdims=True)
            top = jnp.concatenate([jnp.maximum(top[0:part], other), top[part:]], axis=0)
            expo = jnp.exp(found[g] - top)
            total = jnp.sum(expo, axis=-1, keepdims=True)
            added = jnp.dot(expo.astype(jnp.bfloat16), vbuf[pl.ds(0, rows), s], preferred_element_type=F32)
            share = jnp.exp(other - top[0:part])
            first = (added[0:part] + share * vbuf[pl.ds(0, part), s].astype(F32)) / (total[0:part] + share)
            result = jnp.concatenate([first, added[part:] / total[part:]], axis=0).astype(jnp.bfloat16)
            obuf[pl.ds(0, half), s] = result
            total_state = total_state + result.astype(F32) * head_ref[0:1, s]
        return total_state

    for load in loads:
        load.wait()

    def first_phase(c, held):
        held = held + attend_hi(c)

        @pl.when(sends_on)
        def _():
            send_queries(c).wait_recv()
            attend_next(c)

            @pl.when(c == chunks - 1)
            def _():
                send_lse().start()

            send_mixed(c).start()

        return held

    acc[pl.ds(half, half), :] = lax.fori_loop(0, chunks, first_phase, jnp.zeros((half, HEAD), F32))

    stores = [pltpu.make_async_copy(
        obuf.at[pl.ds(half, half)], out_hbm.at[pl.ds(half, half)], store_sem.at[chunks])]
    stores[0].start()

    @pl.when(receives)
    def _():
        send_lse().wait_recv()

    acc_lo = jnp.zeros((half, HEAD), F32)
    for c in range(chunks):
        @pl.when(receives)
        def _():
            send_keys(c).wait_recv()
            send_mixed(c).wait_recv()
        acc_lo = acc_lo + attend_lo(c)
        store = pltpu.make_async_copy(
            obuf.at[pl.ds(0, half), columns(c)], out_hbm.at[pl.ds(0, half), columns(c)], store_sem.at[c])
        store.start()
        stores.append(store)
    acc[pl.ds(0, half), :] = acc_lo

    state = jnp.sum(acc[...].T, axis=0, keepdims=True)
    spot = lax.broadcasted_iota(jnp.int32, (1, rows), 1)
    linked = (pltpu.roll(doc_row, rows - 1, 1) == doc_row) & (spot < rows - 1)
    delta = rew_ref[...] + jnp.where(linked, pltpu.roll(state, rows - 1, 1), F32(0.0)) - state
    gae_local = jnp.sum(table * jnp.broadcast_to(delta, (rows, rows)).T, axis=0, keepdims=True)
    joined = (doc_row == doc_next) & (tp < n_tp - 1)
    coef = jnp.where(joined, jnp.exp((rows - 1 - spot).astype(F32) * decay_log), F32(0.0))
    carry = state[:, 0:1] + gae_decay * gae_local[:, 0:1]

    def summed(x):
        return jnp.broadcast_to(jnp.sum(x, axis=1, keepdims=True), (1, rows))

    rows_out = [summed(gae_local), summed(gae_local * gae_local), summed(coef),
                summed(coef * gae_local), summed(coef * coef), jnp.broadcast_to(carry, (1, rows))]
    for i, value in enumerate(rows_out):
        tp_slot[tp, pl.ds(i, 1), :] = value

    def tp_copy(d):
        return pltpu.make_async_remote_copy(
            src_ref=tp_slot.at[tp], dst_ref=tp_slot.at[tp], send_sem=tp_send.at[d], recv_sem=tp_recv.at[tp],
            device_id={"tp": lax.rem(tp + d, n_tp)}, device_id_type=MESH)

    def tp_wait(peer):
        return pltpu.make_async_remote_copy(
            src_ref=tp_slot.at[peer], dst_ref=tp_slot.at[peer], send_sem=tp_send.at[0], recv_sem=tp_recv.at[peer],
            device_id={"tp": peer}, device_id_type=MESH)

    for d in range(1, n_tp):
        tp_copy(d).start()
    for d in range(1, n_tp):
        tp_wait(lax.rem(tp + d, n_tp)).wait_recv()

    mean_part = jnp.zeros((1, rows), F32)
    square_part = jnp.zeros((1, rows), F32)
    mine = jnp.zeros((1, rows), F32)
    for t in range(n_tp):
        held = tp_slot[t]
        arrived = tp_slot[t + 1][5:6] if t + 1 < n_tp else jnp.zeros((1, rows), F32)
        mean_part = mean_part + held[0:1] + held[2:3] * arrived
        square_part = square_part + held[1:2] + 2.0 * held[3:4] * arrived + held[4:5] * arrived * arrived
        mine = jnp.where(tp == t, arrived, mine)
    gae = gae_local + coef * mine

    sec_slot[sec, pl.ds(0, 1), :] = mean_part
    sec_slot[sec, pl.ds(1, 1), :] = square_part

    def sec_copy(d):
        return pltpu.make_async_remote_copy(
            src_ref=sec_slot.at[sec], dst_ref=sec_slot.at[sec], send_sem=sec_send.at[d], recv_sem=sec_recv.at[sec],
            device_id={"sec": lax.rem(sec + d, n_sec)}, device_id_type=MESH)

    def sec_wait(peer):
        return pltpu.make_async_remote_copy(
            src_ref=sec_slot.at[peer], dst_ref=sec_slot.at[peer], send_sem=sec_send.at[0],
            recv_sem=sec_recv.at[peer], device_id={"sec": peer}, device_id_type=MESH)

    for d in range(1, n_sec):
        sec_copy(d).start()
    for d in range(1, n_sec):
        sec_wait(lax.rem(sec + d, n_sec)).wait_recv()

    total_sum = jnp.zeros((1, rows), F32)
    square_sum = jnp.zeros((1, rows), F32)
    for s in range(n_sec):
        held = sec_slot[s]
        total_sum = total_sum + held[0:1]
        square_sum = square_sum + held[1:2]
    number = n_sec * n_tp * rows
    mean = total_sum / number
    spread = square_sum / number - mean * mean
    adv_ref[...] = (gae - mean) / jnp.sqrt(spread + epsilon)

    for store in stores:
        store.wait()
    for d in range(1, n_tp):
        tp_copy(d).wait_send()
    for d in range(1, n_sec):
        sec_copy(d).wait_send()

    @pl.when(receives)
    def _():
        for c in range(chunks):
            send_queries(c).wait_send()

    @pl.when(sends_on)
    def _():
        for c in range(chunks):
            send_keys(c).wait_send()
            send_mixed(c).wait_send()
        send_lse().wait_send()


def finish(attended_hbm, advantages_ref, out_hbm, adv_ref, buf, read_sem, write_sem):
    pieces = read_sem.shape[0]
    rows = buf.shape[0] // pieces
    reads, writes = [], []
    for i in range(pieces):
        at = pl.ds(i * rows, rows)
        reads.append(pltpu.make_async_copy(attended_hbm.at[at], buf.at[at], read_sem.at[i]))
        writes.append(pltpu.make_async_copy(buf.at[at], out_hbm.at[0, at], write_sem.at[i]))
        reads[i].start()
    adv_ref[...] = advantages_ref[...]
    for i in range(pieces):
        reads[i].wait()
        writes[i].start()
    for write in writes:
        write.wait()


def local(n_sec, n_tp, queries, key_rows, value_rows, doc_ids, rewards, value_head):
    rows, feat = queries.shape[1:]
    part = rows // 4
    chunks = feat // (GROUP * HEAD)
    any_spec = pl.BlockSpec(memory_space=pl.ANY)
    vmem_spec = pl.BlockSpec(memory_space=pltpu.VMEM)
    dma = pltpu.SemaphoreType.DMA
    bf16 = jnp.bfloat16
    attended, advantages = pl.pallas_call(
        functools.partial(kernel, n_sec, n_tp),
        out_shape=(jax.ShapeDtypeStruct((rows, feat), bf16), jax.ShapeDtypeStruct((1, rows), F32)),
        in_specs=[pl.BlockSpec(memory_space=pltpu.HBM)] * 6,
        out_specs=(any_spec, vmem_spec),
        scratch_shapes=[
            pltpu.VMEM((rows, feat), bf16),
            pltpu.VMEM(doc_ids.shape, doc_ids.dtype),
            pltpu.VMEM((1, rows), F32),
            pltpu.VMEM((1, feat), F32),
            pltpu.VMEM((rows, feat), bf16),
            pltpu.VMEM((rows + part, feat), bf16),
            pltpu.VMEM((rows + part, feat), bf16),
            pltpu.VMEM((part, feat), bf16),
            pltpu.VMEM((part, feat), bf16),
            pltpu.VMEM((part, HEAD), F32),
            pltpu.VMEM((part, HEAD), F32),
            pltpu.VMEM((rows, HEAD), F32),
            pltpu.VMEM((n_tp, 8, rows), F32),
            pltpu.VMEM((n_sec, 8, rows), F32),
            dma((6,)), dma((chunks + 1,)),
            dma((chunks,)), dma((chunks,)), dma((chunks,)), dma((chunks,)), dma((chunks,)), dma((chunks,)), dma, dma,
            dma((n_tp,)), dma((n_tp,)), dma((n_sec,)), dma((n_sec,)),
        ],
        compiler_params=pltpu.CompilerParams(collective_id=0, has_side_effects=True),
    )(queries, key_rows, value_rows, doc_ids, rewards, value_head.reshape(1, feat))
    return pl.pallas_call(
        finish,
        out_shape=(jax.ShapeDtypeStruct((1, rows, feat), bf16), jax.ShapeDtypeStruct((1, rows), F32)),
        in_specs=[any_spec, vmem_spec],
        out_specs=(any_spec, vmem_spec),
        scratch_shapes=[pltpu.VMEM((rows, feat), bf16), dma((4,)), dma((4,))],
    )(attended, advantages)


def solution(mesh):
    return jax.shard_map(
        functools.partial(local, mesh.shape["sec"], mesh.shape["tp"]),
        mesh=mesh,
        in_specs=(
            P("sec", "tp", None),
            P("sec", "tp", None),
            P("sec", "tp", None),
            P("sec", None),
            P("sec", "tp"),
            P(),
        ),
        out_specs=(P("sec", "tp", None), P("sec", "tp")),
        check_vma=False,
    )
```

```python
import functools
import math

import jax
import jax.numpy as jnp
from jax import lax
from jax.experimental import pallas as pl
from jax.experimental.pallas import tpu as pltpu
from jax.sharding import PartitionSpec as P

HEAD = 128
GROUP = 8

gae_decay = 0.95
epsilon = 1e-05

MESH = pl.DeviceIdType.MESH
F32 = jnp.float32


def kernel(n_sec, n_tp, q_hbm, k_hbm, v_hbm, doc_hbm, rew_hbm, head_hbm, obuf, adv_ref,
           doc_ref, rew_ref, head_ref, qbuf, kbuf, vbuf, q_in, mixed, lse_out, lse_in, acc, tp_slot, sec_slot,
           load_sem, qsend, qrecv, ksend, krecv, vsend, vrecv, lsend, lrecv,
           tp_send, tp_recv, sec_send, sec_recv):
    rows = qbuf.shape[0]
    feat = qbuf.shape[1]
    half = rows // 2
    part = half // 2
    width = GROUP * HEAD
    chunks = feat // width
    sec = lax.axis_index("sec")
    tp = lax.axis_index("tp")

    barrier = pltpu.get_barrier_semaphore()
    for d in range(1, n_tp):
        pl.semaphore_signal(barrier, inc=1, device_id={"tp": lax.rem(tp + d, n_tp)}, device_id_type=MESH)
    for d in range(1, n_sec):
        pl.semaphore_signal(barrier, inc=1, device_id={"sec": lax.rem(sec + d, n_sec)}, device_id_type=MESH)
    small = [
        pltpu.make_async_copy(doc_hbm, doc_ref, load_sem.at[3]),
        pltpu.make_async_copy(rew_hbm, rew_ref, load_sem.at[4]),
        pltpu.make_async_copy(head_hbm, head_ref, load_sem.at[5]),
    ]
    loads = [
        pltpu.make_async_copy(q_hbm.at[0], qbuf, load_sem.at[0]),
        pltpu.make_async_copy(k_hbm.at[0], kbuf.at[pl.ds(part, rows)], load_sem.at[1]),
        pltpu.make_async_copy(v_hbm.at[0], vbuf.at[pl.ds(part, rows)], load_sem.at[2]),
    ]
    for load in small + loads:
        load.start()

    pl.semaphore_wait(barrier, n_tp + n_sec - 2)

    following = {"tp": lax.rem(tp + 1, n_tp)}
    preceding = {"tp": lax.rem(tp + n_tp - 1, n_tp)}

    def columns(c):
        return pl.ds(pl.multiple_of(c * width, width), width)

    def send_queries(c):
        return pltpu.make_async_remote_copy(
            src_ref=q_hbm.at[0, pl.ds(0, part), columns(c)], dst_ref=q_in.at[:, columns(c)],
            send_sem=qsend.at[c], recv_sem=qrecv.at[c], device_id=preceding, device_id_type=MESH)

    def send_keys(c):
        return pltpu.make_async_remote_copy(
            src_ref=k_hbm.at[0, pl.ds(rows - part, part), columns(c)], dst_ref=kbuf.at[pl.ds(0, part), columns(c)],
            send_sem=ksend.at[c], recv_sem=krecv.at[c], device_id=following, device_id_type=MESH)

    def send_mixed(c):
        return pltpu.make_async_remote_copy(
            src_ref=mixed.at[:, columns(c)], dst_ref=vbuf.at[pl.ds(0, part), columns(c)],
            send_sem=vsend.at[c], recv_sem=vrecv.at[c], device_id=following, device_id_type=MESH)

    def send_lse():
        return pltpu.make_async_remote_copy(
            src_ref=lse_out, dst_ref=lse_in, send_sem=lsend, recv_sem=lrecv,
            device_id=following, device_id_type=MESH)

    sends_on = tp < n_tp - 1
    receives = tp > 0

    @pl.when(receives)
    def _():
        for c in range(chunks):
            send_queries(c).start()

    @pl.when(sends_on)
    def _():
        for c in range(chunks):
            send_keys(c).start()

    @pl.when(tp == 0)
    def _():
        kbuf[pl.ds(0, part), :] = jnp.zeros((part, feat), kbuf.dtype)
        vbuf[pl.ds(0, part), :] = jnp.zeros((part, feat), vbuf.dtype)
        lse_in[...] = jnp.zeros(lse_in.shape, F32)

    lse_out[...] = jnp.zeros(lse_out.shape, F32)

    for load in small:
        load.wait()
    start = pl.multiple_of(tp * rows, rows)
    prev = pl.multiple_of(jnp.maximum(tp - 1, 0) * rows, rows)
    after = pl.multiple_of(jnp.minimum(tp + 1, n_tp - 1) * rows, rows)
    doc_row = doc_ref[0:1, pl.ds(start, rows)].astype(F32)
    doc_prev = doc_ref[0:1, pl.ds(prev, rows)].astype(F32)
    doc_next = doc_ref[0:1, pl.ds(after, rows)].astype(F32)[:, 0:1]
    doc_prev = jnp.where(tp > 0, doc_prev, jnp.float32(-1.0))
    doc_key = jnp.broadcast_to(doc_row, (rows, rows))
    doc_query = doc_key.T
    row_id = lax.broadcasted_iota(jnp.int32, (rows, rows), 0)
    col_id = lax.broadcasted_iota(jnp.int32, (rows, rows), 1)
    same = (col_id <= row_id) & (doc_key == doc_query)
    decay_log = math.log(gae_decay)
    table = jnp.where(same, jnp.exp((row_id - col_id).astype(F32) * decay_log), F32(0.0))
    before = jnp.sum(jnp.where(doc_prev == doc_row[:, 0:1], F32(1.0), F32(0.0)), axis=1, keepdims=True)
    before_next = jnp.sum(jnp.where(doc_row == doc_next, F32(1.0), F32(0.0)), axis=1, keepdims=True)
    given = before > part
    giving = before_next > part
    given_rows = given & (doc_query[0:part, 0:1] == doc_prev[:, rows - 1 : rows])
    doc_keys_prev = jnp.where(given, F32(-1.0), doc_prev)
    lane = lax.broadcasted_iota(jnp.int32, (half, rows), 1)
    line = lax.broadcasted_iota(jnp.int32, (half, rows), 0)
    key_lo = jnp.broadcast_to(
        jnp.where(lane[0:1] < part, pltpu.roll(doc_keys_prev, part, 1), pltpu.roll(doc_row, part, 1)), (half, rows))
    allowed_lo = (lane - part <= line) & (key_lo == doc_query[0:half])
    allowed_hi = (lane <= line + half) & (doc_key[half:] == doc_query[half:])
    allowed_next = jnp.broadcast_to(doc_row == doc_next, (part, rows)) & (lane[0:part] >= half)
    giving_all = jnp.broadcast_to(giving, (part, HEAD))
    head_lane = lax.broadcasted_iota(jnp.int32, (part, HEAD), 1)

    scale = HEAD ** (-0.5)

    def spans_of(c):
        return [pl.ds(pl.multiple_of(c * width + g * HEAD, HEAD), HEAD) for g in range(GROUP)]

    def scores(query, key, allowed):
        raw = lax.dot_general(query, key, (((1,), (1,)), ((), ())), preferred_element_type=F32)
        return jnp.where(allowed, raw * scale, F32(-1e30))

    def attend_hi(c):
        spans = spans_of(c)
        total_state = jnp.zeros((half, HEAD), F32)
        found = [scores(qbuf[pl.ds(half, half), s], kbuf[pl.ds(part, rows), s], allowed_hi) for s in spans]
        for g, s in enumerate(spans):
            top = jnp.max(found[g], axis=-1, keepdims=True)
            expo = jnp.exp(found[g] - top)
            total = jnp.sum(expo, axis=-1, keepdims=True)
            added = jnp.dot(expo.astype(jnp.bfloat16), vbuf[pl.ds(part, rows), s], preferred_element_type=F32)
            result = (added / total).astype(jnp.bfloat16)
            obuf[pl.ds(half, half), s] = result
            total_state = total_state + result.astype(F32) * head_ref[0:1, s]
        return total_state

    def attend_next(c):
        spans = spans_of(c)
        found = [scores(q_in[:, s], kbuf[pl.ds(part, rows), s], allowed_next) for s in spans]
        sums = lse_out[...]
        for g, s in enumerate(spans):
            top = jnp.max(found[g], axis=-1, keepdims=True)
            expo = jnp.exp(found[g] - top)
            total = jnp.sum(expo, axis=-1, keepdims=True)
            added = jnp.dot(expo.astype(jnp.bfloat16), vbuf[pl.ds(part, rows), s], preferred_element_type=F32)
            own = vbuf[pl.ds(rows, part), s]
            mixed[:, s] = jnp.where(giving_all, added / total, own.astype(F32)).astype(jnp.bfloat16)
            sums = jnp.where(head_lane == c * GROUP + g, top + jnp.log(total), sums)
        lse_out[...] = sums

    def attend_lo(c):
        spans = spans_of(c)
        total_state = jnp.zeros((half, HEAD), F32)
        found = [scores(qbuf[pl.ds(0, half), s], kbuf[pl.ds(0, rows), s], allowed_lo) for s in spans]
        for g, s in enumerate(spans):
            h = c * GROUP + g
            other = jnp.where(given_rows, lse_in[:, h : h + 1], F32(-1e30))
            top = jnp.max(found[g], axis=-1, keepdims=True)
            top = jnp.concatenate([jnp.maximum(top[0:part], other), top[part:]], axis=0)
            expo = jnp.exp(found[g] - top)
            total = jnp.sum(expo, axis=-1, keepdims=True)
            added = jnp.dot(expo.astype(jnp.bfloat16), vbuf[pl.ds(0, rows), s], preferred_element_type=F32)
            share = jnp.exp(other - top[0:part])
            first = (added[0:part] + share * vbuf[pl.ds(0, part), s].astype(F32)) / (total[0:part] + share)
            result = jnp.concatenate([first, added[part:] / total[part:]], axis=0).astype(jnp.bfloat16)
            obuf[pl.ds(0, half), s] = result
            total_state = total_state + result.astype(F32) * head_ref[0:1, s]
        return total_state

    for load in loads:
        load.wait()

    def first_phase(c, held):
        held = held + attend_hi(c)

        @pl.when(sends_on)
        def _():
            send_queries(c).wait_recv()
            attend_next(c)

            @pl.when(c == chunks - 1)
            def _():
                send_lse().start()

            send_mixed(c).start()

        return held

    acc[pl.ds(half, half), :] = lax.fori_loop(0, chunks, first_phase, jnp.zeros((half, HEAD), F32))

    @pl.when(receives)
    def _():
        send_lse().wait_recv()

    acc_lo = jnp.zeros((half, HEAD), F32)
    for c in range(chunks):
        @pl.when(receives)
        def _():
            send_keys(c).wait_recv()
            send_mixed(c).wait_recv()
        acc_lo = acc_lo + attend_lo(c)
    acc[pl.ds(0, half), :] = acc_lo

    state = jnp.sum(acc[...].T, axis=0, keepdims=True)
    spot = lax.broadcasted_iota(jnp.int32, (1, rows), 1)
    linked = (pltpu.roll(doc_row, rows - 1, 1) == doc_row) & (spot < rows - 1)
    delta = rew_ref[...] + jnp.where(linked, pltpu.roll(state, rows - 1, 1), F32(0.0)) - state
    gae_local = jnp.sum(table * jnp.broadcast_to(delta, (rows, rows)).T, axis=0, keepdims=True)
    joined = (doc_row == doc_next) & (tp < n_tp - 1)
    coef = jnp.where(joined, jnp.exp((rows - 1 - spot).astype(F32) * decay_log), F32(0.0))
    carry = state[:, 0:1] + gae_decay * gae_local[:, 0:1]

    def summed(x):
        return jnp.broadcast_to(jnp.sum(x, axis=1, keepdims=True), (1, rows))

    rows_out = [summed(gae_local), summed(gae_local * gae_local), summed(coef),
                summed(coef * gae_local), summed(coef * coef), jnp.broadcast_to(carry, (1, rows))]
    for i, value in enumerate(rows_out):
        tp_slot[tp, pl.ds(i, 1), :] = value

    def tp_copy(d):
        return pltpu.make_async_remote_copy(
            src_ref=tp_slot.at[tp], dst_ref=tp_slot.at[tp], send_sem=tp_send.at[d], recv_sem=tp_recv.at[tp],
            device_id={"tp": lax.rem(tp + d, n_tp)}, device_id_type=MESH)

    def tp_wait(peer):
        return pltpu.make_async_remote_copy(
            src_ref=tp_slot.at[peer], dst_ref=tp_slot.at[peer], send_sem=tp_send.at[0], recv_sem=tp_recv.at[peer],
            device_id={"tp": peer}, device_id_type=MESH)

    for d in range(1, n_tp):
        tp_copy(d).start()
    for d in range(1, n_tp):
        tp_wait(lax.rem(tp + d, n_tp)).wait_recv()

    mean_part = jnp.zeros((1, rows), F32)
    square_part = jnp.zeros((1, rows), F32)
    mine = jnp.zeros((1, rows), F32)
    for t in range(n_tp):
        held = tp_slot[t]
        arrived = tp_slot[t + 1][5:6] if t + 1 < n_tp else jnp.zeros((1, rows), F32)
        mean_part = mean_part + held[0:1] + held[2:3] * arrived
        square_part = square_part + held[1:2] + 2.0 * held[3:4] * arrived + held[4:5] * arrived * arrived
        mine = jnp.where(tp == t, arrived, mine)
    gae = gae_local + coef * mine

    sec_slot[sec, pl.ds(0, 1), :] = mean_part
    sec_slot[sec, pl.ds(1, 1), :] = square_part

    def sec_copy(d):
        return pltpu.make_async_remote_copy(
            src_ref=sec_slot.at[sec], dst_ref=sec_slot.at[sec], send_sem=sec_send.at[d], recv_sem=sec_recv.at[sec],
            device_id={"sec": lax.rem(sec + d, n_sec)}, device_id_type=MESH)

    def sec_wait(peer):
        return pltpu.make_async_remote_copy(
            src_ref=sec_slot.at[peer], dst_ref=sec_slot.at[peer], send_sem=sec_send.at[0],
            recv_sem=sec_recv.at[peer], device_id={"sec": peer}, device_id_type=MESH)

    for d in range(1, n_sec):
        sec_copy(d).start()
    for d in range(1, n_sec):
        sec_wait(lax.rem(sec + d, n_sec)).wait_recv()

    total_sum = jnp.zeros((1, rows), F32)
    square_sum = jnp.zeros((1, rows), F32)
    for s in range(n_sec):
        held = sec_slot[s]
        total_sum = total_sum + held[0:1]
        square_sum = square_sum + held[1:2]
    number = n_sec * n_tp * rows
    mean = total_sum / number
    spread = square_sum / number - mean * mean
    adv_ref[...] = (gae - mean) / jnp.sqrt(spread + epsilon)

    for d in range(1, n_tp):
        tp_copy(d).wait_send()
    for d in range(1, n_sec):
        sec_copy(d).wait_send()

    @pl.when(receives)
    def _():
        for c in range(chunks):
            send_queries(c).wait_send()

    @pl.when(sends_on)
    def _():
        for c in range(chunks):
            send_keys(c).wait_send()
            send_mixed(c).wait_send()
        send_lse().wait_send()


def finish(attended_ref, advantages_ref, out_hbm, adv_ref, sem):
    copy = pltpu.make_async_copy(attended_ref, out_hbm.at[0], sem)
    copy.start()
    adv_ref[...] = advantages_ref[...]
    copy.wait()


def local(n_sec, n_tp, queries, key_rows, value_rows, doc_ids, rewards, value_head):
    rows, feat = queries.shape[1:]
    part = rows // 4
    chunks = feat // (GROUP * HEAD)
    any_spec = pl.BlockSpec(memory_space=pl.ANY)
    vmem_spec = pl.BlockSpec(memory_space=pltpu.VMEM)
    dma = pltpu.SemaphoreType.DMA
    bf16 = jnp.bfloat16
    held = [pltpu.with_memory_space_constraint(x, pltpu.HBM) for x in (
        queries, key_rows, value_rows, doc_ids, rewards, value_head.reshape(1, feat))]
    attended, advantages = pl.pallas_call(
        functools.partial(kernel, n_sec, n_tp),
        out_shape=(jax.ShapeDtypeStruct((rows, feat), bf16), jax.ShapeDtypeStruct((1, rows), F32)),
        in_specs=[pl.BlockSpec(memory_space=pltpu.HBM)] * 6,
        out_specs=(vmem_spec, vmem_spec),
        scratch_shapes=[
            pltpu.VMEM(doc_ids.shape, doc_ids.dtype),
            pltpu.VMEM((1, rows), F32),
            pltpu.VMEM((1, feat), F32),
            pltpu.VMEM((rows, feat), bf16),
            pltpu.VMEM((rows + part, feat), bf16),
            pltpu.VMEM((rows + part, feat), bf16),
            pltpu.VMEM((part, feat), bf16),
            pltpu.VMEM((part, feat), bf16),
            pltpu.VMEM((part, HEAD), F32),
            pltpu.VMEM((part, HEAD), F32),
            pltpu.VMEM((rows, HEAD), F32),
            pltpu.VMEM((n_tp, 8, rows), F32),
            pltpu.VMEM((n_sec, 8, rows), F32),
            dma((6,)),
            dma((chunks,)), dma((chunks,)), dma((chunks,)), dma((chunks,)), dma((chunks,)), dma((chunks,)), dma, dma,
            dma((n_tp,)), dma((n_tp,)), dma((n_sec,)), dma((n_sec,)),
        ],
        compiler_params=pltpu.CompilerParams(collective_id=0, has_side_effects=True, vmem_limit_bytes=24 << 20),
    )(*held)
    return pl.pallas_call(
        finish,
        out_shape=(jax.ShapeDtypeStruct((1, rows, feat), bf16), jax.ShapeDtypeStruct((1, rows), F32)),
        in_specs=[vmem_spec, vmem_spec],
        out_specs=(any_spec, vmem_spec),
        scratch_shapes=[dma],
        compiler_params=pltpu.CompilerParams(vmem_limit_bytes=24 << 20),
    )(attended, advantages)


def solution(mesh):
    return jax.shard_map(
        functools.partial(local, mesh.shape["sec"], mesh.shape["tp"]),
        mesh=mesh,
        in_specs=(
            P("sec", "tp", None),
            P("sec", "tp", None),
            P("sec", "tp", None),
            P("sec", None),
            P("sec", "tp"),
            P(),
        ),
        out_specs=(P("sec", "tp", None), P("sec", "tp")),
        check_vma=False,
    )
```

```python
import functools
import math

import jax
import jax.numpy as jnp
from jax import lax
from jax.experimental import pallas as pl
from jax.experimental.pallas import tpu as pltpu
from jax.sharding import PartitionSpec as P

HEAD = 128
GROUP = 4

gae_decay = 0.95
epsilon = 1e-05

MESH = pl.DeviceIdType.MESH
F32 = jnp.float32


def kernel(n_sec, n_tp, q_hbm, k_hbm, v_hbm, doc_hbm, rew_hbm, head_hbm, obuf, adv_ref,
           doc_ref, rew_ref, head_ref, qbuf, kbuf, vbuf, q_in, mixed, lse_out, lse_in, acc, tp_slot, sec_slot,
           load_sem, qsend, qrecv, ksend, krecv, vsend, vrecv, lsend, lrecv,
           tp_send, tp_recv, sec_send, sec_recv):
    rows = qbuf.shape[0]
    feat = qbuf.shape[1]
    half = rows // 2
    part = half // 2
    width = GROUP * HEAD
    chunks = feat // width
    sec = lax.axis_index("sec")
    tp = lax.axis_index("tp")

    barrier = pltpu.get_barrier_semaphore()
    for d in range(1, n_tp):
        pl.semaphore_signal(barrier, inc=1, device_id={"tp": lax.rem(tp + d, n_tp)}, device_id_type=MESH)
    for d in range(1, n_sec):
        pl.semaphore_signal(barrier, inc=1, device_id={"sec": lax.rem(sec + d, n_sec)}, device_id_type=MESH)
    small = [
        pltpu.make_async_copy(doc_hbm, doc_ref, load_sem.at[3]),
        pltpu.make_async_copy(rew_hbm, rew_ref, load_sem.at[4]),
        pltpu.make_async_copy(head_hbm, head_ref, load_sem.at[5]),
    ]
    loads = [
        pltpu.make_async_copy(q_hbm.at[0], qbuf, load_sem.at[0]),
        pltpu.make_async_copy(k_hbm.at[0], kbuf.at[pl.ds(part, rows)], load_sem.at[1]),
        pltpu.make_async_copy(v_hbm.at[0], vbuf.at[pl.ds(part, rows)], load_sem.at[2]),
    ]
    for load in small + loads:
        load.start()

    pl.semaphore_wait(barrier, n_tp + n_sec - 2)

    following = {"tp": lax.rem(tp + 1, n_tp)}
    preceding = {"tp": lax.rem(tp + n_tp - 1, n_tp)}

    def columns(c):
        return pl.ds(pl.multiple_of(c * width, width), width)

    def send_queries(c):
        return pltpu.make_async_remote_copy(
            src_ref=q_hbm.at[0, pl.ds(0, part), columns(c)], dst_ref=q_in.at[:, columns(c)],
            send_sem=qsend.at[c], recv_sem=qrecv.at[c], device_id=preceding, device_id_type=MESH)

    def send_keys(c):
        return pltpu.make_async_remote_copy(
            src_ref=k_hbm.at[0, pl.ds(rows - part, part), columns(c)], dst_ref=kbuf.at[pl.ds(0, part), columns(c)],
            send_sem=ksend.at[c], recv_sem=krecv.at[c], device_id=following, device_id_type=MESH)

    def send_mixed(c):
        return pltpu.make_async_remote_copy(
            src_ref=mixed.at[:, columns(c)], dst_ref=vbuf.at[pl.ds(0, part), columns(c)],
            send_sem=vsend.at[c], recv_sem=vrecv.at[c], device_id=following, device_id_type=MESH)

    def send_lse():
        return pltpu.make_async_remote_copy(
            src_ref=lse_out, dst_ref=lse_in, send_sem=lsend, recv_sem=lrecv,
            device_id=following, device_id_type=MESH)

    sends_on = tp < n_tp - 1
    receives = tp > 0

    @pl.when(receives)
    def _():
        for c in range(chunks):
            send_queries(c).start()

    @pl.when(sends_on)
    def _():
        for c in range(chunks):
            send_keys(c).start()

    @pl.when(tp == 0)
    def _():
        kbuf[pl.ds(0, part), :] = jnp.zeros((part, feat), kbuf.dtype)
        vbuf[pl.ds(0, part), :] = jnp.zeros((part, feat), vbuf.dtype)
        lse_in[...] = jnp.zeros(lse_in.shape, F32)

    lse_out[...] = jnp.zeros(lse_out.shape, F32)

    for load in small:
        load.wait()
    start = pl.multiple_of(tp * rows, rows)
    prev = pl.multiple_of(jnp.maximum(tp - 1, 0) * rows, rows)
    after = pl.multiple_of(jnp.minimum(tp + 1, n_tp - 1) * rows, rows)
    doc_row = doc_ref[0:1, pl.ds(start, rows)].astype(F32)
    doc_prev = doc_ref[0:1, pl.ds(prev, rows)].astype(F32)
    doc_next = doc_ref[0:1, pl.ds(after, rows)].astype(F32)[:, 0:1]
    doc_prev = jnp.where(tp > 0, doc_prev, jnp.float32(-1.0))
    doc_key = jnp.broadcast_to(doc_row, (rows, rows))
    doc_query = doc_key.T
    row_id = lax.broadcasted_iota(jnp.int32, (rows, rows), 0)
    col_id = lax.broadcasted_iota(jnp.int32, (rows, rows), 1)
    same = (col_id <= row_id) & (doc_key == doc_query)
    decay_log = math.log(gae_decay)
    table = jnp.where(same, jnp.exp((row_id - col_id).astype(F32) * decay_log), F32(0.0))
    before = jnp.sum(jnp.where(doc_prev == doc_row[:, 0:1], F32(1.0), F32(0.0)), axis=1, keepdims=True)
    before_next = jnp.sum(jnp.where(doc_row == doc_next, F32(1.0), F32(0.0)), axis=1, keepdims=True)
    given = before > part
    giving = before_next > part
    given_rows = given & (doc_query[0:part, 0:1] == doc_prev[:, rows - 1 : rows])
    doc_keys_prev = jnp.where(given, F32(-1.0), doc_prev)
    lane = lax.broadcasted_iota(jnp.int32, (half, rows), 1)
    line = lax.broadcasted_iota(jnp.int32, (half, rows), 0)
    key_lo = jnp.broadcast_to(
        jnp.where(lane[0:1] < part, pltpu.roll(doc_keys_prev, part, 1), pltpu.roll(doc_row, part, 1)), (half, rows))
    allowed_lo = (lane - part <= line) & (key_lo == doc_query[0:half])
    allowed_hi = (lane <= line + half) & (doc_key[half:] == doc_query[half:])
    allowed_next = jnp.broadcast_to(doc_row == doc_next, (part, rows)) & (lane[0:part] >= half)
    giving_all = jnp.broadcast_to(giving, (part, HEAD))
    head_lane = lax.broadcasted_iota(jnp.int32, (part, HEAD), 1)

    scale = HEAD ** (-0.5)

    def spans_of(c):
        return [pl.ds(pl.multiple_of(c * width + g * HEAD, HEAD), HEAD) for g in range(GROUP)]

    def scores(query, key, allowed):
        raw = lax.dot_general(query, key, (((1,), (1,)), ((), ())), preferred_element_type=F32)
        return jnp.where(allowed, raw * scale, F32(-1e30))

    def attend_hi(c):
        spans = spans_of(c)
        total_state = jnp.zeros((half, HEAD), F32)
        found = [scores(qbuf[pl.ds(half, half), s], kbuf[pl.ds(part, rows), s], allowed_hi) for s in spans]
        for g, s in enumerate(spans):
            top = jnp.max(found[g], axis=-1, keepdims=True)
            expo = jnp.exp(found[g] - top)
            total = jnp.sum(expo, axis=-1, keepdims=True)
            added = jnp.dot(expo.astype(jnp.bfloat16), vbuf[pl.ds(part, rows), s], preferred_element_type=F32)
            result = (added / total).astype(jnp.bfloat16)
            obuf[pl.ds(half, half), s] = result
            total_state = total_state + result.astype(F32) * head_ref[0:1, s]
        return total_state

    def attend_next(c):
        spans = spans_of(c)
        found = [scores(q_in[:, s], kbuf[pl.ds(part, rows), s], allowed_next) for s in spans]
        sums = lse_out[...]
        for g, s in enumerate(spans):
            top = jnp.max(found[g], axis=-1, keepdims=True)
            expo = jnp.exp(found[g] - top)
            total = jnp.sum(expo, axis=-1, keepdims=True)
            added = jnp.dot(expo.astype(jnp.bfloat16), vbuf[pl.ds(part, rows), s], preferred_element_type=F32)
            own = vbuf[pl.ds(rows, part), s]
            mixed[:, s] = jnp.where(giving_all, added / total, own.astype(F32)).astype(jnp.bfloat16)
            sums = jnp.where(head_lane == c * GROUP + g, top + jnp.log(total), sums)
        lse_out[...] = sums

    def attend_lo(c):
        spans = spans_of(c)
        total_state = jnp.zeros((half, HEAD), F32)
        found = [scores(qbuf[pl.ds(0, half), s], kbuf[pl.ds(0, rows), s], allowed_lo) for s in spans]
        for g, s in enumerate(spans):
            h = c * GROUP + g
            other = jnp.where(given_rows, lse_in[:, h : h + 1], F32(-1e30))
            top = jnp.max(found[g], axis=-1, keepdims=True)
            top = jnp.concatenate([jnp.maximum(top[0:part], other), top[part:]], axis=0)
            expo = jnp.exp(found[g] - top)
            total = jnp.sum(expo, axis=-1, keepdims=True)
            added = jnp.dot(expo.astype(jnp.bfloat16), vbuf[pl.ds(0, rows), s], preferred_element_type=F32)
            share = jnp.exp(other - top[0:part])
            first = (added[0:part] + share * vbuf[pl.ds(0, part), s].astype(F32)) / (total[0:part] + share)
            result = jnp.concatenate([first, added[part:] / total[part:]], axis=0).astype(jnp.bfloat16)
            obuf[pl.ds(0, half), s] = result
            total_state = total_state + result.astype(F32) * head_ref[0:1, s]
        return total_state

    for load in loads:
        load.wait()

    def first_phase(c, held):
        held = held + attend_hi(c)

        @pl.when(sends_on)
        def _():
            send_queries(c).wait_recv()
            attend_next(c)

            @pl.when(c == chunks - 1)
            def _():
                send_lse().start()

            send_mixed(c).start()

        return held

    acc[pl.ds(half, half), :] = lax.fori_loop(0, chunks, first_phase, jnp.zeros((half, HEAD), F32))

    @pl.when(receives)
    def _():
        send_lse().wait_recv()

    acc_lo = jnp.zeros((half, HEAD), F32)
    for c in range(chunks):
        @pl.when(receives)
        def _():
            send_keys(c).wait_recv()
            send_mixed(c).wait_recv()
        acc_lo = acc_lo + attend_lo(c)
    acc[pl.ds(0, half), :] = acc_lo

    state = jnp.sum(acc[...].T, axis=0, keepdims=True)
    spot = lax.broadcasted_iota(jnp.int32, (1, rows), 1)
    linked = (pltpu.roll(doc_row, rows - 1, 1) == doc_row) & (spot < rows - 1)
    delta = rew_ref[...] + jnp.where(linked, pltpu.roll(state, rows - 1, 1), F32(0.0)) - state
    gae_local = jnp.sum(table * jnp.broadcast_to(delta, (rows, rows)).T, axis=0, keepdims=True)
    joined = (doc_row == doc_next) & (tp < n_tp - 1)
    coef = jnp.where(joined, jnp.exp((rows - 1 - spot).astype(F32) * decay_log), F32(0.0))
    carry = state[:, 0:1] + gae_decay * gae_local[:, 0:1]

    def summed(x):
        return jnp.broadcast_to(jnp.sum(x, axis=1, keepdims=True), (1, rows))

    rows_out = [summed(gae_local), summed(gae_local * gae_local), summed(coef),
                summed(coef * gae_local), summed(coef * coef), jnp.broadcast_to(carry, (1, rows))]
    for i, value in enumerate(rows_out):
        tp_slot[tp, pl.ds(i, 1), :] = value

    def tp_copy(d):
        return pltpu.make_async_remote_copy(
            src_ref=tp_slot.at[tp], dst_ref=tp_slot.at[tp], send_sem=tp_send.at[d], recv_sem=tp_recv.at[tp],
            device_id={"tp": lax.rem(tp + d, n_tp)}, device_id_type=MESH)

    def tp_wait(peer):
        return pltpu.make_async_remote_copy(
            src_ref=tp_slot.at[peer], dst_ref=tp_slot.at[peer], send_sem=tp_send.at[0], recv_sem=tp_recv.at[peer],
            device_id={"tp": peer}, device_id_type=MESH)

    for d in range(1, n_tp):
        tp_copy(d).start()
    for d in range(1, n_tp):
        tp_wait(lax.rem(tp + d, n_tp)).wait_recv()

    mean_part = jnp.zeros((1, rows), F32)
    square_part = jnp.zeros((1, rows), F32)
    mine = jnp.zeros((1, rows), F32)
    for t in range(n_tp):
        held = tp_slot[t]
        arrived = tp_slot[t + 1][5:6] if t + 1 < n_tp else jnp.zeros((1, rows), F32)
        mean_part = mean_part + held[0:1] + held[2:3] * arrived
        square_part = square_part + held[1:2] + 2.0 * held[3:4] * arrived + held[4:5] * arrived * arrived
        mine = jnp.where(tp == t, arrived, mine)
    gae = gae_local + coef * mine

    sec_slot[sec, pl.ds(0, 1), :] = mean_part
    sec_slot[sec, pl.ds(1, 1), :] = square_part

    def sec_copy(d):
        return pltpu.make_async_remote_copy(
            src_ref=sec_slot.at[sec], dst_ref=sec_slot.at[sec], send_sem=sec_send.at[d], recv_sem=sec_recv.at[sec],
            device_id={"sec": lax.rem(sec + d, n_sec)}, device_id_type=MESH)

    def sec_wait(peer):
        return pltpu.make_async_remote_copy(
            src_ref=sec_slot.at[peer], dst_ref=sec_slot.at[peer], send_sem=sec_send.at[0],
            recv_sem=sec_recv.at[peer], device_id={"sec": peer}, device_id_type=MESH)

    for d in range(1, n_sec):
        sec_copy(d).start()
    for d in range(1, n_sec):
        sec_wait(lax.rem(sec + d, n_sec)).wait_recv()

    total_sum = jnp.zeros((1, rows), F32)
    square_sum = jnp.zeros((1, rows), F32)
    for s in range(n_sec):
        held = sec_slot[s]
        total_sum = total_sum + held[0:1]
        square_sum = square_sum + held[1:2]
    number = n_sec * n_tp * rows
    mean = total_sum / number
    spread = square_sum / number - mean * mean
    adv_ref[...] = (gae - mean) / jnp.sqrt(spread + epsilon)

    for d in range(1, n_tp):
        tp_copy(d).wait_send()
    for d in range(1, n_sec):
        sec_copy(d).wait_send()

    @pl.when(receives)
    def _():
        for c in range(chunks):
            send_queries(c).wait_send()

    @pl.when(sends_on)
    def _():
        for c in range(chunks):
            send_keys(c).wait_send()
            send_mixed(c).wait_send()
        send_lse().wait_send()


def finish(attended_ref, advantages_ref, out_hbm, adv_ref, sem):
    pieces = sem.shape[0]
    rows = attended_ref.shape[0] // pieces
    writes = []
    for i in range(pieces):
        at = pl.ds(i * rows, rows)
        writes.append(pltpu.make_async_copy(attended_ref.at[at], out_hbm.at[0, at], sem.at[i]))
        writes[i].start()
    adv_ref[...] = advantages_ref[...]
    for write in writes:
        write.wait()


def local(n_sec, n_tp, queries, key_rows, value_rows, doc_ids, rewards, value_head):
    rows, feat = queries.shape[1:]
    part = rows // 4
    chunks = feat // (GROUP * HEAD)
    any_spec = pl.BlockSpec(memory_space=pl.ANY)
    vmem_spec = pl.BlockSpec(memory_space=pltpu.VMEM)
    dma = pltpu.SemaphoreType.DMA
    bf16 = jnp.bfloat16
    held = [pltpu.with_memory_space_constraint(x, pltpu.HBM) for x in (
        queries, key_rows, value_rows, doc_ids, rewards, value_head.reshape(1, feat))]
    attended, advantages = pl.pallas_call(
        functools.partial(kernel, n_sec, n_tp),
        out_shape=(jax.ShapeDtypeStruct((rows, feat), bf16), jax.ShapeDtypeStruct((1, rows), F32)),
        in_specs=[pl.BlockSpec(memory_space=pltpu.HBM)] * 6,
        out_specs=(vmem_spec, vmem_spec),
        scratch_shapes=[
            pltpu.VMEM(doc_ids.shape, doc_ids.dtype),
            pltpu.VMEM((1, rows), F32),
            pltpu.VMEM((1, feat), F32),
            pltpu.VMEM((rows, feat), bf16),
            pltpu.VMEM((rows + part, feat), bf16),
            pltpu.VMEM((rows + part, feat), bf16),
            pltpu.VMEM((part, feat), bf16),
            pltpu.VMEM((part, feat), bf16),
            pltpu.VMEM((part, HEAD), F32),
            pltpu.VMEM((part, HEAD), F32),
            pltpu.VMEM((rows, HEAD), F32),
            pltpu.VMEM((n_tp, 8, rows), F32),
            pltpu.VMEM((n_sec, 8, rows), F32),
            dma((6,)),
            dma((chunks,)), dma((chunks,)), dma((chunks,)), dma((chunks,)), dma((chunks,)), dma((chunks,)), dma, dma,
            dma((n_tp,)), dma((n_tp,)), dma((n_sec,)), dma((n_sec,)),
        ],
        compiler_params=pltpu.CompilerParams(collective_id=0, has_side_effects=True, vmem_limit_bytes=24 << 20),
    )(*held)
    return pl.pallas_call(
        finish,
        out_shape=(jax.ShapeDtypeStruct((1, rows, feat), bf16), jax.ShapeDtypeStruct((1, rows), F32)),
        in_specs=[vmem_spec, vmem_spec],
        out_specs=(any_spec, vmem_spec),
        scratch_shapes=[dma((4,))],
        compiler_params=pltpu.CompilerParams(vmem_limit_bytes=24 << 20),
    )(attended, advantages)


def solution(mesh):
    return jax.shard_map(
        functools.partial(local, mesh.shape["sec"], mesh.shape["tp"]),
        mesh=mesh,
        in_specs=(
            P("sec", "tp", None),
            P("sec", "tp", None),
            P("sec", "tp", None),
            P("sec", None),
            P("sec", "tp"),
            P(),
        ),
        out_specs=(P("sec", "tp", None), P("sec", "tp")),
        check_vma=False,
    )
```
